32 devices in a mesh: grp: 2 (over x), ep: 8 (over z, y), dp: 2 (over core).
Axes of the slice: x: 2, y: 2, z: 4, core: 2. Of those that a mesh axis runs over, the one named last changes fastest.
Arguments:
- tokens: bfloat16 [2, 1024, 2048], P(None, ('grp', 'ep', 'dp')), parts along dimension 1, may hold values from -6 to 6
- norm_gain: float32 [2048], replicated, may hold values from 0.25 to 1.75
- expert_ids: int32 [2, 1024, 8], P(None, ('grp', 'ep', 'dp')), parts along dimension 1, may hold values from 0 to 15, all different within a row; in each aligned block of 32 rows (0 to 31, 32 to 63, ..., all dimensions but the last counted through in order) at most 24 rows name the same one
- gate_probs: float32 [2, 1024, 8], P(None, ('grp', 'ep', 'dp')), parts along dimension 1, may hold values from 0.05 to 1
- expert_weights: bfloat16 [16, 3, 2048, 768], P(('ep', 'dp')), may hold values from -0.125 to 0.125
Outputs:
- combined: bfloat16 [2, 1024, 2048], P(None, ('grp', 'ep', 'dp')), parts along dimension 1
The draws below stay inside these ranges and needn't reach their ends.
There are 2 independent parts, one for each index of `grp`. The reference program is written for one: setup_inputs(seed, part) draws one part's arguments, and reference() takes and returns one part's arrays. A program takes and returns all parts, laid end to end along the dimension named above; an argument that names none is the same for every part. Nothing has to cross between parts.
Inputs may be any that keep to these rules, and one draw needn't show every extreme that they name: `expert_ids`: each token names 8 different experts. In each step the 32 tokens of one device (aligned blocks of 32 rows) name any one expert at most 24 times, a bound that some block reaches; every expert is named somewhere.
All inputs are finite; a program needn't handle non-finite values.
Results may differ from the reference program's by a relative error of at most 0.0072.
Values may be sent and summed in bfloat16 or wider, within the bound.
A program may use at most 128 MiB of HBM per device.

```python
import math
import jax
import jax.numpy as jnp
import numpy as np
from jax import lax

D = 2048
FF = 768
TOP = 8
STEPS = 2
TOK_DEV = 32
EXPERTS = 16
TOKENS = 512
CAP = 24


def levels(rng, shape, shards, low, high):
    def one(dim, parts):
        heights = jax.random.uniform(jax.random.fold_in(jax.random.fold_in(rng, 6), dim), (parts,), jnp.float32, low / len(shards), high / len(shards))
        return jnp.repeat(jnp.exp(heights), shape[dim] // parts).reshape((-1,) + (1,) * (len(shape) - dim - 1))

    level = one(*shards[0])
    for cut in shards[1:]:
        level = level * one(*cut)
    return level


def assign_block(key, own, number, rows, count, top, most, lean):
    sequence = jax.random.permutation(key, count)
    crowded, usual = shares(count, rows * top, most, lean, True), shares(count, rows * top, most, lean, False)
    places = jnp.arange(count)

    def named(lengths, turn):
        used = int((lengths > 0).sum())
        fixed = max(1, used // 4)
        shifted = fixed + (places - fixed + turn * (used - fixed)) % max(1, count - fixed)
        return jnp.zeros((count,), jnp.int32).at[sequence[jnp.where(places < fixed, places, shifted)]].set(jnp.asarray(lengths, jnp.int32))

    lengths = jnp.where(number % 4 == 0, named(crowded, number // 4), named(usual, number - number // 4 - 1))
    mixed = jax.random.permutation(jax.random.fold_in(own, 3), count)
    giver, taker = mixed[0:count // 2 * 2:2], mixed[1:count // 2 * 2:2]
    room = jnp.minimum(lengths[giver] - 1, most - lengths[taker]) // 2
    room = jnp.where((giver == sequence[0]) | (taker == sequence[0]) | (lengths[taker] == 0), 0, jnp.maximum(room, 0))
    shifted = jax.random.randint(jax.random.fold_in(own, 4), (count // 2,), 0, 1 << 20) % (room + 1)
    lengths = lengths.at[giver].add(-shifted).at[taker].add(shifted)
    members = jnp.searchsorted(jnp.cumsum(lengths), jnp.arange(rows * top), side="right").astype(jnp.int32)
    table = members.reshape(top, rows).T
    table = table[jax.random.permutation(jax.random.fold_in(own, 1), rows)]
    turn = jax.random.randint(jax.random.fold_in(own, 2), (rows, 1), 0, top)
    return jnp.take_along_axis(table, (jnp.arange(top)[None, :] + turn) % top, axis=1)


def shares(count, total, limit, slope, full):
    weights = [(1 << 20) // math.isqrt(rank ** slope) + 1 for rank in range(1, count + 1)]
    largest = limit if full else min(limit, max(-(-total // count), total * weights[0] // sum(weights)))
    least = 1 if total - largest >= count - 1 else 0
    holding, surplus = [largest] + [least] * (count - 1), total - largest - least * (count - 1)
    while surplus > 0:
        candidates = [i for i in range(1, count) if holding[i] < largest] or [i for i in range(1, count) if holding[i] < limit]
        pool, budget = sum([weights[i] for i in candidates]), surplus
        for i in candidates:
            addition = min(limit - holding[i], max(1, budget * weights[i] // pool), surplus)
            holding[i] = holding[i] + addition
            surplus = surplus - addition
    return np.array(holding)


def scatter_about(rng, shape, scale, bound, pieces=(), held_as=jnp.bfloat16):
    values = scale * jax.random.normal(rng, shape, jnp.float32)
    if pieces:
        values = values * levels(rng, shape, pieces, -0.22, 0.18)
    return jnp.clip(values, -bound, bound).astype(held_as)


def setup_inputs(seed: int = 0, part: int = 0) -> dict:
    streams_of = jax.random.split(jax.random.key(seed), 6)
    part_splits = jax.random.split(jax.random.fold_in(streams_of[5], part), 6)
    tokens = scatter_about(part_splits[0], (STEPS, TOKENS, D), 1.0, 6.0, ((1, 16),))
    norm_gain = jnp.clip(1.0 + 0.15 * jax.random.normal(streams_of[1], (D,), jnp.float32), 0.25, 1.75)
    expert_ids_keys = jax.random.split(jax.random.fold_in(part_splits[2], 1), STEPS * TOKENS // TOK_DEV)
    expert_ids_turns = jax.random.permutation(jax.random.fold_in(part_splits[2], 3), STEPS * TOKENS // TOK_DEV)
    expert_ids = jax.vmap(lambda own, number: assign_block(jax.random.fold_in(part_splits[2], 2), own, number, TOK_DEV, EXPERTS, TOP, CAP, 2))(expert_ids_keys, expert_ids_turns).reshape((STEPS, TOKENS, TOP))
    gate_probs = jnp.clip(jnp.exp(math.log(1.0) - 2.9957323 * jax.random.uniform(part_splits[3], (STEPS, TOKENS, TOP), jnp.float32) ** levels(part_splits[3], (STEPS, TOKENS, TOP), ((1, 16),), -0.2, 0.2)), 0.05, 1.0)
    expert_weights = scatter_about(streams_of[4], (EXPERTS, 3, D, FF), D ** -0.5, 0.125, ((0, 16),))
    return dict(tokens=tokens, norm_gain=norm_gain, expert_ids=expert_ids, gate_probs=gate_probs, expert_weights=expert_weights)


def norm_rows(hidden_rows, norm_gain):
    values = hidden_rows.astype(jnp.float32)
    inverse_rms = lax.rsqrt(lax.optimization_barrier(jnp.mean(values * values, axis=-1, keepdims=True)) + 1e-06)
    return (values * inverse_rms * norm_gain).astype(jnp.bfloat16)

def expert_rows(row_block, weights):
    gate_part = jnp.dot(row_block, weights[0], preferred_element_type=jnp.float32)
    up_part = jnp.dot(row_block, weights[1], preferred_element_type=jnp.float32)
    hidden = (jax.nn.silu(gate_part) * up_part).astype(jnp.bfloat16)
    return lax.dot_general(hidden, weights[2], (((1,), (1,)), ((), ())), preferred_element_type=jnp.float32)

def one_step(step_tokens, norm_gain, step_ids, step_probs, expert_weights):
    normed = norm_rows(step_tokens, norm_gain)
    share = step_probs / lax.optimization_barrier(jnp.sum(step_probs, axis=1, keepdims=True))
    flat_ids = step_ids.reshape(-1).astype(jnp.int32)
    flat_share = share.reshape(-1)
    row_limit = EXPERTS * CAP

    def per_expert(running, expert):
        chosen = (flat_ids == expert).astype(jnp.int32)
        picked = jnp.argsort(1 - chosen, stable=True)[:row_limit].astype(jnp.int32)
        valid = jnp.arange(row_limit, dtype=jnp.int32) < jnp.sum(chosen)
        token_index = (picked // TOP).astype(jnp.int32)
        picked_rows = normed[token_index]
        produced = expert_rows(picked_rows, expert_weights[expert]).astype(jnp.bfloat16)
        weighted = jnp.where(valid[:, None], flat_share[picked][:, None] * produced.astype(jnp.float32), jnp.zeros((), jnp.float32))
        return (running.at[token_index].add(weighted), None)
    start_sum = jnp.zeros(normed.shape, jnp.float32)
    total_sum, _ = lax.scan(per_expert, start_sum, jnp.arange(EXPERTS, dtype=jnp.int32))
    return total_sum.astype(jnp.bfloat16)

def reference(tokens, norm_gain, expert_ids, gate_probs, expert_weights):
    results = []
    for decode_step in range(STEPS):
        results.append(one_step(tokens[decode_step], norm_gain, expert_ids[decode_step], gate_probs[decode_step], expert_weights))
    return jnp.stack(results)
```

```python
import jax
import jax.numpy as jnp
from jax import lax
from jax.sharding import PartitionSpec as P


def norm_rows(hidden_rows, norm_gain):
    values = hidden_rows.astype(jnp.float32)
    inverse_rms = lax.rsqrt(jnp.mean(values * values, axis=-1, keepdims=True) + 1e-06)
    return (values * inverse_rms * norm_gain).astype(jnp.bfloat16)


def expert_rows(row_block, weights):
    gate_part = jnp.dot(row_block, weights[0], preferred_element_type=jnp.float32)
    up_part = jnp.dot(row_block, weights[1], preferred_element_type=jnp.float32)
    hidden = (jax.nn.silu(gate_part) * up_part).astype(jnp.bfloat16)
    return lax.dot_general(
        hidden, weights[2], (((1,), (1,)), ((), ())), preferred_element_type=jnp.float32
    )


def shards(tokens, norm_gain, expert_ids, gate_probs, expert_weights):
    axes = ("ep", "dp")
    experts = lax.axis_size("ep") * lax.axis_size("dp")
    me = lax.axis_index(axes)
    steps_total, tok_count, width = tokens.shape
    rows = steps_total * tok_count
    normed = norm_rows(tokens.reshape(rows, width), norm_gain)
    share = gate_probs / jnp.sum(gate_probs, axis=-1, keepdims=True)
    hits = expert_ids[..., None] == lax.broadcasted_iota(jnp.int32, (1, 1, 1, experts), 3)
    dense_share = jnp.sum(jnp.where(hits, share[..., None], 0.0), axis=2).reshape(rows, experts)
    all_rows = lax.all_gather(normed, axes, tiled=True)
    all_share = lax.all_gather(dense_share, axes, tiled=True)
    mine = lax.broadcasted_iota(jnp.int32, (1, experts), 1) == me
    row_share = jnp.sum(jnp.where(mine, all_share, 0.0), axis=1, keepdims=True)
    expert_out = expert_rows(all_rows, expert_weights[0])
    weighted = (row_share * expert_out).astype(jnp.bfloat16)
    combined = lax.psum_scatter(weighted, axes, scatter_dimension=0, tiled=True)
    return combined.reshape(steps_total, tok_count, width)


def solution(mesh):
    in_specs = (
        P(None, ("grp", "ep", "dp"), None),
        P(),
        P(None, ("grp", "ep", "dp"), None),
        P(None, ("grp", "ep", "dp"), None),
        P(("ep", "dp"), None, None, None),
    )
    out_specs = P(None, ("grp", "ep", "dp"), None)
    return jax.shard_map(shards, mesh=mesh, in_specs=in_specs, out_specs=out_specs, check_vma=False)
```

```python
import functools

import jax
import jax.numpy as jnp
from jax import lax
from jax.experimental import pallas as pl
from jax.experimental.pallas import tpu as pltpu
from jax.sharding import PartitionSpec as P

NZ = 4
NY = 2
LANES = 128
B_LAG, D_LAG, E_LAG, END_LAG, INNER_LAG = 1, 2, 3, 6, 8


def norm_rows(hidden_rows, norm_gain):
    values = hidden_rows.astype(jnp.float32)
    inverse_rms = lax.rsqrt(jnp.mean(values * values, axis=-1, keepdims=True) + 1e-06)
    return (values * inverse_rms * norm_gain).astype(jnp.bfloat16)


def expert_rows(row_block, weights):
    gate_part = jnp.dot(row_block, weights[0], preferred_element_type=jnp.float32)
    up_part = jnp.dot(row_block, weights[1], preferred_element_type=jnp.float32)
    hidden = (jax.nn.silu(gate_part) * up_part).astype(jnp.bfloat16)
    return lax.dot_general(
        hidden, weights[2], (((1,), (1,)), ((), ())), preferred_element_type=jnp.float32
    )


def gather_scatter_form(tokens, norm_gain, expert_ids, gate_probs, expert_weights):
    axes = ("ep", "dp")
    experts = lax.axis_size("ep") * lax.axis_size("dp")
    me = lax.axis_index(axes)
    steps_total, tok_count, width = tokens.shape
    rows = steps_total * tok_count
    normed = norm_rows(tokens.reshape(rows, width), norm_gain)
    share = gate_probs / jnp.sum(gate_probs, axis=-1, keepdims=True)
    hits = expert_ids[..., None] == lax.broadcasted_iota(jnp.int32, (1, 1, 1, experts), 3)
    dense_share = jnp.sum(jnp.where(hits, share[..., None], 0.0), axis=2).reshape(rows, experts)
    all_rows = lax.all_gather(normed, axes, tiled=True)
    all_share = lax.all_gather(dense_share, axes, tiled=True)
    mine = lax.broadcasted_iota(jnp.int32, (1, experts), 1) == me
    row_share = jnp.sum(jnp.where(mine, all_share, 0.0), axis=1, keepdims=True)
    expert_out = expert_rows(all_rows, expert_weights[0])
    weighted = (row_share * expert_out).astype(jnp.bfloat16)
    combined = lax.psum_scatter(weighted, axes, scatter_dimension=0, tiled=True)
    return combined.reshape(steps_total, tok_count, width)


def near_order(z, j):
    high = z // 2
    inner = z + high * (3 - 2 * z)
    first = (3 - j) // 3
    second = (j + 2) // 3 * ((4 - j) // 3)
    k = j + inner * (first - second)
    return k + high * (3 - 2 * k)


def chain_order(z, g):
    high = z // 2
    inner = z + high * (3 - 2 * z)
    k = (1 - inner) * (g + 1) + inner * ((g + 2) % 4)
    return k + high * (3 - 2 * k)


def moe_kernel(
    tok_ref, gain_ref, ids_ref, prob_ref, w_hbm, out_ref,
    x, wv, hid, ob, sr, ys, yr, zs, zr,
    w_sem, x_recv, x_send, c_recv, c_send, y_recv, y_send, z_recv, z_send,
):
    steps, toks, width = tok_ref.shape
    top = ids_ref.shape[2]
    ff = wv.shape[2]
    experts = lax.axis_size("ep") * lax.axis_size("dp")
    ep = lax.axis_index("ep")
    c = lax.axis_index("dp")
    z = ep // NY
    y = ep % NY
    me = ep * 2 + c
    groups = steps * NZ

    sib = {"ep": ep, "dp": 1 - c}
    ynb = {"ep": z * NY + 1 - y, "dp": c}
    zup = {"ep": (z + 1) % NZ * NY + y, "dp": c}
    zdn = {"ep": (z + NZ - 1) % NZ * NY + y, "dp": c}
    can_up = z < NZ - 1
    can_dn = z > 0
    g_lag = jnp.where(can_up & can_dn, INNER_LAG, END_LAG)

    for i in range(3):
        pltpu.make_async_copy(w_hbm.at[0, i], wv.at[i], w_sem.at[i]).start()

    barrier = pltpu.get_barrier_semaphore()
    for peer in (sib, ynb):
        pl.semaphore_signal(barrier, inc=1, device_id=peer)

    @pl.when(can_up)
    def _():
        pl.semaphore_signal(barrier, inc=1, device_id=zup)

    @pl.when(can_dn)
    def _():
        pl.semaphore_signal(barrier, inc=1, device_id=zdn)

    def prepare(s):
        x[s, z, c, y, :, :width] = norm_rows(tok_ref[s], gain_ref[...])
        probs = prob_ref[s]
        share = probs / jnp.sum(probs, axis=1, keepdims=True)
        ids = ids_ref[s]
        lane = lax.broadcasted_iota(jnp.int32, (toks, LANES), 1)
        both = jnp.zeros((toks, LANES), jnp.float32)
        for i in range(top):
            named = ids[:, i : i + 1]
            both = jnp.where(
                (lane == named) | (lane == named + experts), share[:, i : i + 1], both
            )
        high = both.astype(jnp.bfloat16).astype(jnp.float32)
        x[s, z, c, y, :, width:] = jnp.where(lane < experts, high, both - high).astype(jnp.bfloat16)

    prepare(0)
    pl.semaphore_wait(barrier, 2 + (z + NZ - 1) // NZ + (2 * (NZ - 1) - z) // NZ)

    def x_copy(s, k, col, row, send, peer):
        block = x.at[s, k, col, row]
        return pltpu.make_async_remote_copy(
            block, block, x_send.at[s, k, send], x_recv.at[s, k, col, row], device_id=peer
        )

    def relay_copies(s, k, act):
        @pl.when((k <= z) & can_up)
        def _():
            act(x_copy(s, k, c, y, 0, zup))

        @pl.when((k >= z) & can_dn)
        def _():
            act(x_copy(s, k, c, y, 1, zdn))

        act(x_copy(s, k, c, y, 2, ynb))
        act(x_copy(s, k, c, y, 3, sib))

    def y_relay(s, k):
        return x_copy(s, k, c, 1 - y, 4, sib)

    def c_copy(s, k):
        t = s * NZ + k
        return pltpu.make_async_remote_copy(
            ob.at[t, 1 - c], sr.at[t], c_send.at[t], c_recv.at[t], device_id=sib
        )

    def y_copy(s, k):
        t = s * NZ + k
        return pltpu.make_async_remote_copy(
            ys.at[t], yr.at[t], y_send.at[t], y_recv.at[t], device_id=ynb
        )

    def z_copy(s, k, way, peer):
        t = s * NZ + k
        return pltpu.make_async_remote_copy(
            zs.at[t], zr.at[s, way, k], z_send.at[t], z_recv.at[s, way, k], device_id=peer
        )

    def start(copy):
        copy.start()

    def finish(copy):
        copy.wait_send()

    def phase_a(t):
        s, j = t // NZ, t % NZ
        k = near_order(z, j)

        @pl.when(j > 0)
        def _():
            x_copy(s, k, c, y, 2, ynb).wait_recv()

        relay_copies(s, k, start)

    def phase_b(t):
        s, j = t // NZ, t % NZ
        k = near_order(z, j)
        x_copy(s, k, c, 1 - y, 2, ynb).wait_recv()
        y_relay(s, k).start()

    def phase_d(t):
        s, j = t // NZ, t % NZ
        k = near_order(z, j)

        @pl.when(t == 0)
        def _():
            for i in range(3):
                pltpu.make_async_copy(w_hbm.at[0, i], wv.at[i], w_sem.at[i]).wait()

        for row in range(NY):
            x_copy(s, k, 1 - c, row, 3, sib).wait_recv()
        rows = 2 * NY * toks
        lane = lax.broadcasted_iota(jnp.int32, (rows, LANES), 1)
        pieces = x[s, k, :, :, :, width:].reshape(rows, LANES).astype(jnp.float32)
        mine = (lane == me) | (lane == me + experts)
        share = jnp.sum(jnp.where(mine, pieces, 0.0), axis=1, keepdims=True)
        block = x[s, k, :, :, :, :width].reshape(rows, width)
        tile = 256
        for f in range(0, ff, tile):
            gate = jnp.dot(block, wv[0, :, f : f + tile], preferred_element_type=jnp.float32)
            up = jnp.dot(block, wv[1, :, f : f + tile], preferred_element_type=jnp.float32)
            hid[:, f : f + tile] = (gate / (1.0 + jnp.exp(-gate)) * up).astype(jnp.bfloat16)
        hidden = hid[...]
        for d in range(0, width, tile):
            part = lax.dot_general(
                hidden, wv[2, d : d + tile, :], (((1,), (1,)), ((), ())),
                preferred_element_type=jnp.float32,
            )
            ob[s * NZ + k, :, :, :, d : d + tile] = (
                (share * part).astype(jnp.bfloat16).reshape(2, NY, toks, tile)
            )
        c_copy(s, k).start()

    def f32(value):
        return value.astype(jnp.float32)

    def phase_e(t):
        s, j = t // NZ, t % NZ
        k = near_order(z, j)
        n = s * NZ + k
        c_copy(s, k).wait_recv()
        ys[n] = (f32(ob[n, c, 1 - y]) + f32(sr[n, 1 - y])).astype(jnp.bfloat16)
        y_copy(s, k).start()

    def chip_sum(s, k):
        n = s * NZ + k
        return f32(ob[n, c, y]) + f32(sr[n, y]) + f32(yr[n])

    def phase_g(s, g):
        k = chain_order(z, g)
        n = s * NZ + k
        y_copy(s, k).wait_recv()

        @pl.when(k > z)
        def _():
            @pl.when(can_dn)
            def _():
                z_copy(s, k, 0, zup).wait_recv()
                zs[n] = (chip_sum(s, k) + f32(zr[s, 0, k])).astype(jnp.bfloat16)

            @pl.when(z == 0)
            def _():
                zs[n] = chip_sum(s, k).astype(jnp.bfloat16)

            z_copy(s, k, 0, zup).start()

        @pl.when(k < z)
        def _():
            @pl.when(can_up)
            def _():
                z_copy(s, k, 1, zdn).wait_recv()
                zs[n] = (chip_sum(s, k) + f32(zr[s, 1, k])).astype(jnp.bfloat16)

            @pl.when(z == NZ - 1)
            def _():
                zs[n] = chip_sum(s, k).astype(jnp.bfloat16)

            z_copy(s, k, 1, zdn).start()

    def phase_h(s):
        y_copy(s, z).wait_recv()

        @pl.when(z == 0)
        def _():
            z_copy(s, z, 1, zdn).wait_recv()
            out_ref[s] = (chip_sum(s, z) + f32(zr[s, 1, z])).astype(jnp.bfloat16)

        @pl.when(z == NZ - 1)
        def _():
            z_copy(s, z, 0, zup).wait_recv()
            out_ref[s] = (chip_sum(s, z) + f32(zr[s, 0, z])).astype(jnp.bfloat16)

        @pl.when(can_up & can_dn)
        def _():
            z_copy(s, z, 0, zup).wait_recv()
            z_copy(s, z, 1, zdn).wait_recv()
            out_ref[s] = (
                chip_sum(s, z) + f32(zr[s, 0, z]) + f32(zr[s, 1, z])
            ).astype(jnp.bfloat16)

    def slot_body(slot, carry):
        @pl.when(slot < groups)
        def _():
            phase_a(slot)

        @pl.when(slot == 0)
        def _():
            for s in range(1, steps):
                prepare(s)

        @pl.when((slot >= B_LAG) & (slot < groups + B_LAG))
        def _():
            phase_b(slot - B_LAG)

        @pl.when((slot >= D_LAG) & (slot < groups + D_LAG))
        def _():
            phase_d(slot - D_LAG)

        @pl.when((slot >= E_LAG) & (slot < groups + E_LAG))
        def _():
            phase_e(slot - E_LAG)

        @pl.when((slot >= g_lag) & (slot < groups + g_lag))
        def _():
            t = slot - g_lag
            s, g = t // NZ, t % NZ

            @pl.when(g < NZ - 1)
            def _():
                phase_g(s, g)

            @pl.when(g == NZ - 1)
            def _():
                phase_h(s)

        return carry

    lax.fori_loop(0, groups + INNER_LAG, slot_body, 0)

    def drain(t, carry):
        s, k = t // NZ, t % NZ
        relay_copies(s, k, finish)
        y_relay(s, k).wait_send()
        c_copy(s, k).wait_send()
        y_copy(s, k).wait_send()

        @pl.when(k != z)
        def _():
            z_copy(s, k, 0, zup).wait_send()

        return carry

    lax.fori_loop(0, groups, drain, 0)


def kernel_form(tokens, norm_gain, expert_ids, gate_probs, expert_weights):
    steps, toks, width = tokens.shape
    ff = expert_weights.shape[3]
    groups = steps * NZ
    half = jnp.bfloat16
    vmem = pl.BlockSpec(memory_space=pltpu.VMEM)
    dma = pltpu.SemaphoreType.DMA
    rows = groups * 4 * toks
    return pl.pallas_call(
        moe_kernel,
        out_shape=jax.ShapeDtypeStruct((steps, toks, width), half),
        in_specs=[vmem, vmem, vmem, vmem, pl.BlockSpec(memory_space=pl.ANY)],
        out_specs=vmem,
        scratch_shapes=[
            pltpu.VMEM((steps, NZ, 2, NY, toks, width + LANES), half),
            pltpu.VMEM((3, width, ff), half),
            pltpu.VMEM((4 * toks, ff), half),
            pltpu.VMEM((groups, 2, NY, toks, width), half),
            pltpu.VMEM((groups, NY, toks, width), half),
            pltpu.VMEM((groups, toks, width), half),
            pltpu.VMEM((groups, toks, width), half),
            pltpu.VMEM((groups, toks, width), half),
            pltpu.VMEM((steps, 2, NZ, toks, width), half),
            dma((3,)),
            dma((steps, NZ, 2, NY)),
            dma((steps, NZ, 5)),
            dma((groups,)),
            dma((groups,)),
            dma((groups,)),
            dma((groups,)),
            dma((steps, 2, NZ)),
            dma((groups,)),
        ],
        compiler_params=pltpu.CompilerParams(
            collective_id=0, has_side_effects=True, vmem_limit_bytes=48 * 1024 * 1024
        ),
        cost_estimate=pl.CostEstimate(
            flops=6 * rows * width * ff, bytes_accessed=6 * width * ff, transcendentals=rows * ff
        ),
    )(tokens, norm_gain.reshape(1, width), expert_ids, gate_probs, expert_weights)


def solution(mesh):
    in_specs = (
        P(None, ("grp", "ep", "dp"), None),
        P(),
        P(None, ("grp", "ep", "dp"), None),
        P(None, ("grp", "ep", "dp"), None),
        P(("ep", "dp"), None, None, None),
    )
    out_specs = P(None, ("grp", "ep", "dp"), None)
    small = mesh.shape["ep"] == NZ * NY and mesh.shape["dp"] == 2
    shards = kernel_form if small else gather_scatter_form
    return jax.shard_map(shards, mesh=mesh, in_specs=in_specs, out_specs=out_specs, check_vma=False)
```

```python
import functools

import jax
import jax.numpy as jnp
from jax import lax
from jax.experimental import pallas as pl
from jax.experimental.pallas import tpu as pltpu
from jax.sharding import PartitionSpec as P

NZ = 4
NY = 2
LANES = 128
B_LAG, D_LAG, E_LAG, G_LAG = 1, 2, 3, 4


def norm_rows(hidden_rows, norm_gain):
    values = hidden_rows.astype(jnp.float32)
    inverse_rms = lax.rsqrt(jnp.mean(values * values, axis=-1, keepdims=True) + 1e-06)
    return (values * inverse_rms * norm_gain).astype(jnp.bfloat16)


def expert_rows(row_block, weights):
    gate_part = jnp.dot(row_block, weights[0], preferred_element_type=jnp.float32)
    up_part = jnp.dot(row_block, weights[1], preferred_element_type=jnp.float32)
    hidden = (jax.nn.silu(gate_part) * up_part).astype(jnp.bfloat16)
    return lax.dot_general(
        hidden, weights[2], (((1,), (1,)), ((), ())), preferred_element_type=jnp.float32
    )


def gather_scatter_form(tokens, norm_gain, expert_ids, gate_probs, expert_weights):
    axes = ("ep", "dp")
    experts = lax.axis_size("ep") * lax.axis_size("dp")
    me = lax.axis_index(axes)
    steps_total, tok_count, width = tokens.shape
    rows = steps_total * tok_count
    normed = norm_rows(tokens.reshape(rows, width), norm_gain)
    share = gate_probs / jnp.sum(gate_probs, axis=-1, keepdims=True)
    hits = expert_ids[..., None] == lax.broadcasted_iota(jnp.int32, (1, 1, 1, experts), 3)
    dense_share = jnp.sum(jnp.where(hits, share[..., None], 0.0), axis=2).reshape(rows, experts)
    all_rows = lax.all_gather(normed, axes, tiled=True)
    all_share = lax.all_gather(dense_share, axes, tiled=True)
    mine = lax.broadcasted_iota(jnp.int32, (1, experts), 1) == me
    row_share = jnp.sum(jnp.where(mine, all_share, 0.0), axis=1, keepdims=True)
    expert_out = expert_rows(all_rows, expert_weights[0])
    weighted = (row_share * expert_out).astype(jnp.bfloat16)
    combined = lax.psum_scatter(weighted, axes, scatter_dimension=0, tiled=True)
    return combined.reshape(steps_total, tok_count, width)


def near_order(z, j):
    high = z // 2
    inner = z + high * (3 - 2 * z)
    first = (3 - j) // 3
    second = (j + 2) // 3 * ((4 - j) // 3)
    k = j + inner * (first - second)
    return k + high * (3 - 2 * k)


def moe_kernel(
    tok_ref, gain_ref, ids_ref, prob_ref, w_hbm, out_ref,
    x, wv, hid, ob, sr, ys, yr, zs, zr,
    w_sem, x_recv, x_send, c_recv, c_send, y_recv, y_send, z_recv, z_send,
):
    steps, toks, width = tok_ref.shape
    top = ids_ref.shape[2]
    ff = wv.shape[2]
    experts = lax.axis_size("ep") * lax.axis_size("dp")
    ep = lax.axis_index("ep")
    c = lax.axis_index("dp")
    z = ep // NY
    y = ep % NY
    me = ep * 2 + c
    groups = steps * NZ

    sib = {"ep": ep, "dp": 1 - c}
    ynb = {"ep": z * NY + 1 - y, "dp": c}
    zup = {"ep": (z + 1) % NZ * NY + y, "dp": c}
    zdn = {"ep": (z + NZ - 1) % NZ * NY + y, "dp": c}
    can_up = z < NZ - 1
    can_dn = z > 0

    for i in range(3):
        pltpu.make_async_copy(w_hbm.at[0, i], wv.at[i], w_sem.at[i]).start()

    barrier = pltpu.get_barrier_semaphore()
    for peer in (sib, ynb):
        pl.semaphore_signal(barrier, inc=1, device_id=peer)

    for far in range(1, NZ):
        peer = {"ep": (z + far) % NZ * NY + y, "dp": c}
        pl.semaphore_signal(barrier, inc=1, device_id=peer)

    def prepare(s):
        x[s, z, c, y, :, :width] = norm_rows(tok_ref[s], gain_ref[...])
        probs = prob_ref[s]
        share = probs / jnp.sum(probs, axis=1, keepdims=True)
        ids = ids_ref[s]
        lane = lax.broadcasted_iota(jnp.int32, (toks, LANES), 1)
        both = jnp.zeros((toks, LANES), jnp.float32)
        for i in range(top):
            named = ids[:, i : i + 1]
            both = jnp.where(
                (lane == named) | (lane == named + experts), share[:, i : i + 1], both
            )
        high = both.astype(jnp.bfloat16).astype(jnp.float32)
        x[s, z, c, y, :, width:] = jnp.where(lane < experts, high, both - high).astype(jnp.bfloat16)

    prepare(0)
    pl.semaphore_wait(barrier, NZ + 1)

    def x_copy(s, k, col, row, send, peer):
        block = x.at[s, k, col, row]
        return pltpu.make_async_remote_copy(
            block, block, x_send.at[s, k, send], x_recv.at[s, k, col, row], device_id=peer
        )

    def relay_copies(s, k, act):
        @pl.when((k <= z) & can_up)
        def _():
            act(x_copy(s, k, c, y, 0, zup))

        @pl.when((k >= z) & can_dn)
        def _():
            act(x_copy(s, k, c, y, 1, zdn))

        @pl.when((c == 0) | (k == z))
        def _():
            act(x_copy(s, k, c, y, 2, ynb))

        act(x_copy(s, k, c, y, 3, sib))

    def far_copies(s, k, act):
        @pl.when((c == 1) & (k <= z) & can_up)
        def _():
            act(x_copy(s, k, c, 1 - y, 4, zup))

        @pl.when((c == 1) & (k >= z) & can_dn)
        def _():
            act(x_copy(s, k, c, 1 - y, 5, zdn))

        act(x_copy(s, k, c, 1 - y, 6, sib))

    def c_copy(s, k):
        t = s * NZ + k
        return pltpu.make_async_remote_copy(
            ob.at[t, 1 - c], sr.at[t], c_send.at[t], c_recv.at[t], device_id=sib
        )

    def y_copy(s, k):
        t = s * NZ + k
        return pltpu.make_async_remote_copy(
            ys.at[t], yr.at[t], y_send.at[t], y_recv.at[t], device_id=ynb
        )

    def z_copy(s, k, place):
        t = s * NZ + k
        return pltpu.make_async_remote_copy(
            zs.at[t], zr.at[s, place], z_send.at[t], z_recv.at[s, place],
            device_id={"ep": k * NY + y, "dp": c},
        )

    def start(copy):
        copy.start()

    def finish(copy):
        copy.wait_send()

    def phase_a(t):
        j, s = t // steps, t % steps
        k = near_order(z, j)

        @pl.when(j > 0)
        def _():
            x_copy(s, k, c, y, 2, ynb).wait_recv()

        relay_copies(s, k, start)

    def phase_b(t):
        j, s = t // steps, t % steps
        k = near_order(z, j)
        x_copy(s, k, c, 1 - y, 2, ynb).wait_recv()
        far_copies(s, k, start)

    def phase_d(t):
        j, s = t // steps, t % steps
        k = near_order(z, j)

        @pl.when(t == 0)
        def _():
            for i in range(3):
                pltpu.make_async_copy(w_hbm.at[0, i], wv.at[i], w_sem.at[i]).wait()

        for row in range(NY):
            x_copy(s, k, 1 - c, row, 3, sib).wait_recv()
        rows = 2 * NY * toks
        lane = lax.broadcasted_iota(jnp.int32, (rows, LANES), 1)
        pieces = x[s, k, :, :, :, width:].reshape(rows, LANES).astype(jnp.float32)
        mine = (lane == me) | (lane == me + experts)
        share = jnp.sum(jnp.where(mine, pieces, 0.0), axis=1, keepdims=True)
        block = x[s, k, :, :, :, :width].reshape(rows, width)
        tile = 256
        for f in range(0, ff, tile):
            gate = jnp.dot(block, wv[0, :, f : f + tile], preferred_element_type=jnp.float32)
            up = jnp.dot(block, wv[1, :, f : f + tile], preferred_element_type=jnp.float32)
            hid[:, f : f + tile] = (gate / (1.0 + jnp.exp(-gate)) * up).astype(jnp.bfloat16)
        hidden = hid[...]
        for d in range(0, width, tile):
            part = lax.dot_general(
                hidden, wv[2, d : d + tile, :], (((1,), (1,)), ((), ())),
                preferred_element_type=jnp.float32,
            )
            ob[s * NZ + k, :, :, :, d : d + tile] = (
                (share * part).astype(jnp.bfloat16).reshape(2, NY, toks, tile)
            )
        c_copy(s, k).start()

    def f32(value):
        return value.astype(jnp.float32)

    def phase_e(t):
        j, s = t // steps, t % steps
        k = near_order(z, j)
        n = s * NZ + k
        c_copy(s, k).wait_recv()
        ys[n] = (f32(ob[n, c, 1 - y]) + f32(sr[n, 1 - y])).astype(jnp.bfloat16)
        y_copy(s, k).start()

    def chip_sum(s, k):
        n = s * NZ + k
        return f32(ob[n, c, y]) + f32(sr[n, y]) + f32(yr[n])

    def phase_g(t):
        j, s = t // steps, t % steps
        k = near_order(z, j)

        @pl.when(j > 0)
        def _():
            y_copy(s, k).wait_recv()
            zs[s * NZ + k] = chip_sum(s, k).astype(jnp.bfloat16)
            z_copy(s, k, z).start()

    def phase_h(s):
        y_copy(s, z).wait_recv()
        zr[s, z] = jnp.zeros(zr.shape[2:], zr.dtype)
        for far in range(1, NZ):
            z_copy(s, z, (z + far) % NZ).wait_recv()
        total = chip_sum(s, z)
        for place in range(NZ):
            total = total + f32(zr[s, place])
        out_ref[s] = total.astype(jnp.bfloat16)

    def slot_body(slot, carry):
        @pl.when(slot < groups)
        def _():
            phase_a(slot)

        @pl.when(slot == 0)
        def _():
            for s in range(1, steps):
                prepare(s)

        @pl.when((slot >= B_LAG) & (slot < groups + B_LAG))
        def _():
            phase_b(slot - B_LAG)

        @pl.when((slot >= D_LAG) & (slot < groups + D_LAG))
        def _():
            phase_d(slot - D_LAG)

        @pl.when((slot >= E_LAG) & (slot < groups + E_LAG))
        def _():
            phase_e(slot - E_LAG)

        @pl.when((slot >= G_LAG) & (slot < groups + G_LAG))
        def _():
            phase_g(slot - G_LAG)

        return carry

    lax.fori_loop(0, groups + G_LAG, slot_body, 0)
    for s in range(steps):
        phase_h(s)

    def drain(t, carry):
        s, k = t // NZ, t % NZ
        relay_copies(s, k, finish)
        far_copies(s, k, finish)
        c_copy(s, k).wait_send()
        y_copy(s, k).wait_send()

        @pl.when(k != z)
        def _():
            z_copy(s, k, z).wait_send()

        return carry

    lax.fori_loop(0, groups, drain, 0)


def kernel_form(tokens, norm_gain, expert_ids, gate_probs, expert_weights):
    steps, toks, width = tokens.shape
    ff = expert_weights.shape[3]
    groups = steps * NZ
    half = jnp.bfloat16
    vmem = pl.BlockSpec(memory_space=pltpu.VMEM)
    dma = pltpu.SemaphoreType.DMA
    rows = groups * 4 * toks
    return pl.pallas_call(
        moe_kernel,
        out_shape=jax.ShapeDtypeStruct((steps, toks, width), half),
        in_specs=[vmem, vmem, vmem, vmem, pl.BlockSpec(memory_space=pl.ANY)],
        out_specs=vmem,
        scratch_shapes=[
            pltpu.VMEM((steps, NZ, 2, NY, toks, width + LANES), half),
            pltpu.VMEM((3, width, ff), half),
            pltpu.VMEM((4 * toks, ff), half),
            pltpu.VMEM((groups, 2, NY, toks, width), half),
            pltpu.VMEM((groups, NY, toks, width), half),
            pltpu.VMEM((groups, toks, width), half),
            pltpu.VMEM((groups, toks, width), half),
            pltpu.VMEM((groups, toks, width), half),
            pltpu.VMEM((steps, NZ, toks, width), half),
            dma((3,)),
            dma((steps, NZ, 2, NY)),
            dma((steps, NZ, 7)),
            dma((groups,)),
            dma((groups,)),
            dma((groups,)),
            dma((groups,)),
            dma((steps, NZ)),
            dma((groups,)),
        ],
        compiler_params=pltpu.CompilerParams(
            collective_id=0, has_side_effects=True, vmem_limit_bytes=48 * 1024 * 1024
        ),
        cost_estimate=pl.CostEstimate(
            flops=6 * rows * width * ff, bytes_accessed=6 * width * ff, transcendentals=rows * ff
        ),
    )(tokens, norm_gain.reshape(1, width), expert_ids, gate_probs, expert_weights)


def solution(mesh):
    in_specs = (
        P(None, ("grp", "ep", "dp"), None),
        P(),
        P(None, ("grp", "ep", "dp"), None),
        P(None, ("grp", "ep", "dp"), None),
        P(("ep", "dp"), None, None, None),
    )
    out_specs = P(None, ("grp", "ep", "dp"), None)
    small = mesh.shape["ep"] == NZ * NY and mesh.shape["dp"] == 2
    shards = kernel_form if small else gather_scatter_form
    return jax.shard_map(shards, mesh=mesh, in_specs=in_specs, out_specs=out_specs, check_vma=False)
```

```python
import functools

import jax
import jax.numpy as jnp
from jax import lax
from jax.experimental import pallas as pl
from jax.experimental.pallas import tpu as pltpu
from jax.sharding import PartitionSpec as P

NZ = 4
NY = 2
LANES = 128
B_LAG, D_LAG, E_LAG, G_LAG = 1, 2, 3, 4


def norm_rows(hidden_rows, norm_gain):
    values = hidden_rows.astype(jnp.float32)
    inverse_rms = lax.rsqrt(jnp.mean(values * values, axis=-1, keepdims=True) + 1e-06)
    return (values * inverse_rms * norm_gain).astype(jnp.bfloat16)


def expert_rows(row_block, weights):
    gate_part = jnp.dot(row_block, weights[0], preferred_element_type=jnp.float32)
    up_part = jnp.dot(row_block, weights[1], preferred_element_type=jnp.float32)
    hidden = (jax.nn.silu(gate_part) * up_part).astype(jnp.bfloat16)
    return lax.dot_general(
        hidden, weights[2], (((1,), (1,)), ((), ())), preferred_element_type=jnp.float32
    )


def gather_scatter_form(tokens, norm_gain, expert_ids, gate_probs, expert_weights):
    axes = ("ep", "dp")
    experts = lax.axis_size("ep") * lax.axis_size("dp")
    me = lax.axis_index(axes)
    steps_total, tok_count, width = tokens.shape
    rows = steps_total * tok_count
    normed = norm_rows(tokens.reshape(rows, width), norm_gain)
    share = gate_probs / jnp.sum(gate_probs, axis=-1, keepdims=True)
    hits = expert_ids[..., None] == lax.broadcasted_iota(jnp.int32, (1, 1, 1, experts), 3)
    dense_share = jnp.sum(jnp.where(hits, share[..., None], 0.0), axis=2).reshape(rows, experts)
    all_rows = lax.all_gather(normed, axes, tiled=True)
    all_share = lax.all_gather(dense_share, axes, tiled=True)
    mine = lax.broadcasted_iota(jnp.int32, (1, experts), 1) == me
    row_share = jnp.sum(jnp.where(mine, all_share, 0.0), axis=1, keepdims=True)
    expert_out = expert_rows(all_rows, expert_weights[0])
    weighted = (row_share * expert_out).astype(jnp.bfloat16)
    combined = lax.psum_scatter(weighted, axes, scatter_dimension=0, tiled=True)
    return combined.reshape(steps_total, tok_count, width)


def near_order(z, j):
    high = z // 2
    inner = z + high * (3 - 2 * z)
    first = (3 - j) // 3
    second = (j + 2) // 3 * ((4 - j) // 3)
    k = j + inner * (first - second)
    return k + high * (3 - 2 * k)


def moe_kernel(
    tok_ref, gain_ref, ids_ref, prob_ref, w_hbm, out_ref,
    x, wv, hid, ob, sr, ys, yr, zs, zr,
    w_sem, x_recv, x_send, c_recv, c_send, y_recv, y_send, z_recv, z_send,
):
    steps, toks, width = tok_ref.shape
    top = ids_ref.shape[2]
    ff = wv.shape[2]
    experts = lax.axis_size("ep") * lax.axis_size("dp")
    ep = lax.axis_index("ep")
    c = lax.axis_index("dp")
    z = ep // NY
    y = ep % NY
    me = ep * 2 + c
    groups = steps * NZ

    sib = {"ep": ep, "dp": 1 - c}
    ynb = {"ep": z * NY + 1 - y, "dp": c}
    zup = {"ep": (z + 1) % NZ * NY + y, "dp": c}
    zdn = {"ep": (z + NZ - 1) % NZ * NY + y, "dp": c}
    can_up = z < NZ - 1
    can_dn = z > 0

    for i in range(3):
        pltpu.make_async_copy(w_hbm.at[0, i], wv.at[i], w_sem.at[i]).start()

    barrier = pltpu.get_barrier_semaphore()
    for peer in (sib, ynb):
        pl.semaphore_signal(barrier, inc=1, device_id=peer)

    for far in range(1, NZ):
        peer = {"ep": (z + far) % NZ * NY + y, "dp": c}
        pl.semaphore_signal(barrier, inc=1, device_id=peer)

    def prepare(s):
        x[s, z, c, y, :, :width] = norm_rows(tok_ref[s], gain_ref[...])
        probs = prob_ref[s]
        share = probs / jnp.sum(probs, axis=1, keepdims=True)
        ids = ids_ref[s]
        lane = lax.broadcasted_iota(jnp.int32, (toks, LANES), 1)
        both = jnp.zeros((toks, LANES), jnp.float32)
        for i in range(top):
            named = ids[:, i : i + 1]
            both = jnp.where(
                (lane == named) | (lane == named + experts), share[:, i : i + 1], both
            )
        high = both.astype(jnp.bfloat16).astype(jnp.float32)
        x[s, z, c, y, :, width:] = jnp.where(lane < experts, high, both - high).astype(jnp.bfloat16)

    prepare(0)
    pl.semaphore_wait(barrier, NZ + 1)

    def x_copy(s, k, col, row, send, peer):
        block = x.at[s, k, col, row]
        return pltpu.make_async_remote_copy(
            block, block, x_send.at[s, k, send], x_recv.at[s, k, col, row], device_id=peer
        )

    def relay_copies(s, k, act):
        @pl.when((k <= z) & can_up)
        def _():
            act(x_copy(s, k, c, y, 0, zup))

        @pl.when((k >= z) & can_dn)
        def _():
            act(x_copy(s, k, c, y, 1, zdn))

        @pl.when((c == 0) | (k == z))
        def _():
            act(x_copy(s, k, c, y, 2, ynb))

        act(x_copy(s, k, c, y, 3, sib))

    def far_copies(s, k, act):
        @pl.when((c == 1) & (k <= z) & can_up)
        def _():
            act(x_copy(s, k, c, 1 - y, 4, zup))

        @pl.when((c == 1) & (k >= z) & can_dn)
        def _():
            act(x_copy(s, k, c, 1 - y, 5, zdn))

        act(x_copy(s, k, c, 1 - y, 6, sib))

    def c_copy(s, k):
        t = s * NZ + k
        return pltpu.make_async_remote_copy(
            ob.at[t, 1 - c], sr.at[t], c_send.at[t], c_recv.at[t], device_id=sib
        )

    def y_copy(s, k):
        t = s * NZ + k
        return pltpu.make_async_remote_copy(
            ys.at[t], yr.at[t], y_send.at[t], y_recv.at[t], device_id=ynb
        )

    def z_copy(s, k, place):
        t = s * NZ + k
        return pltpu.make_async_remote_copy(
            zs.at[t], zr.at[s, place], z_send.at[t], z_recv.at[s, place],
            device_id={"ep": k * NY + y, "dp": c},
        )

    def start(copy):
        copy.start()

    def finish(copy):
        copy.wait_send()

    def phase_a(t):
        j, s = t // steps, t % steps
        k = near_order(z, j)

        @pl.when(j > 0)
        def _():
            x_copy(s, k, c, y, 2, ynb).wait_recv()

        relay_copies(s, k, start)

    def phase_b(t):
        j, s = t // steps, t % steps
        k = near_order(z, j)
        x_copy(s, k, c, 1 - y, 2, ynb).wait_recv()
        far_copies(s, k, start)

    def phase_d(t):
        j, s = t // steps, t % steps
        k = near_order(z, j)

        @pl.when(t == 0)
        def _():
            for i in range(3):
                pltpu.make_async_copy(w_hbm.at[0, i], wv.at[i], w_sem.at[i]).wait()

        for row in range(NY):
            x_copy(s, k, 1 - c, row, 3, sib).wait_recv()
        rows = 2 * NY * toks
        lane = lax.broadcasted_iota(jnp.int32, (rows, LANES), 1)
        pieces = x[s, k, :, :, :, width:].reshape(rows, LANES).astype(jnp.float32)
        mine = (lane == me) | (lane == me + experts)
        share = jnp.sum(jnp.where(mine, pieces, 0.0), axis=1, keepdims=True)
        block = x[s, k, :, :, :, :width].reshape(rows, width)
        tile = 256
        for f in range(0, ff, tile):
            gate = jnp.dot(block, wv[0, :, f : f + tile], preferred_element_type=jnp.float32)
            up = jnp.dot(block, wv[1, :, f : f + tile], preferred_element_type=jnp.float32)
            hid[:, f : f + tile] = (gate / (1.0 + jnp.exp(-gate)) * up).astype(jnp.bfloat16)
        hidden = hid[...]
        for d in range(0, width, tile):
            part = lax.dot_general(
                hidden, wv[2, d : d + tile, :], (((1,), (1,)), ((), ())),
                preferred_element_type=jnp.float32,
            )
            ob[s * NZ + k, :, :, :, d : d + tile] = (
                (share * part).astype(jnp.bfloat16).reshape(2, NY, toks, tile)
            )
        c_copy(s, k).start()

    def f32(value):
        return value.astype(jnp.float32)

    def phase_e(t):
        j, s = t // steps, t % steps
        k = near_order(z, j)
        n = s * NZ + k
        c_copy(s, k).wait_recv()
        ys[n] = (f32(ob[n, c, 1 - y]) + f32(sr[n, 1 - y])).astype(jnp.bfloat16)
        y_copy(s, k).start()

    def chip_sum(s, k):
        n = s * NZ + k
        return f32(ob[n, c, y]) + f32(sr[n, y]) + f32(yr[n])

    def phase_g(t):
        j, s = t // steps, t % steps
        k = near_order(z, j)

        @pl.when(j > 0)
        def _():
            y_copy(s, k).wait_recv()
            zs[s * NZ + k] = chip_sum(s, k).astype(jnp.bfloat16)
            z_copy(s, k, z).start()

    def phase_h(s):
        y_copy(s, z).wait_recv()
        zr[s, z] = jnp.zeros(zr.shape[2:], zr.dtype)
        for far in range(1, NZ):
            z_copy(s, z, (z + far) % NZ).wait_recv()
        total = chip_sum(s, z)
        for place in range(NZ):
            total = total + f32(zr[s, place])
        out_ref[s] = total.astype(jnp.bfloat16)

    def slot_body(slot, carry):
        @pl.when(slot < groups)
        def _():
            phase_a(slot)

        @pl.when(slot == 0)
        def _():
            for s in range(1, steps):
                prepare(s)

        @pl.when((slot >= B_LAG) & (slot < groups + B_LAG))
        def _():
            phase_b(slot - B_LAG)

        @pl.when((slot >= G_LAG) & (slot < groups + G_LAG))
        def _():
            phase_g(slot - G_LAG)

        @pl.when((slot >= E_LAG) & (slot < groups + E_LAG))
        def _():
            phase_e(slot - E_LAG)

        @pl.when((slot >= D_LAG) & (slot < groups + D_LAG))
        def _():
            phase_d(slot - D_LAG)

        return carry

    lax.fori_loop(0, groups + G_LAG, slot_body, 0)
    for s in range(steps):
        phase_h(s)

    def drain(t, carry):
        s, k = t // NZ, t % NZ
        relay_copies(s, k, finish)
        far_copies(s, k, finish)
        c_copy(s, k).wait_send()
        y_copy(s, k).wait_send()

        @pl.when(k != z)
        def _():
            z_copy(s, k, z).wait_send()

        return carry

    lax.fori_loop(0, groups, drain, 0)


def kernel_form(tokens, norm_gain, expert_ids, gate_probs, expert_weights):
    steps, toks, width = tokens.shape
    ff = expert_weights.shape[3]
    groups = steps * NZ
    half = jnp.bfloat16
    vmem = pl.BlockSpec(memory_space=pltpu.VMEM)
    dma = pltpu.SemaphoreType.DMA
    rows = groups * 4 * toks
    return pl.pallas_call(
        moe_kernel,
        out_shape=jax.ShapeDtypeStruct((steps, toks, width), half),
        in_specs=[vmem, vmem, vmem, vmem, pl.BlockSpec(memory_space=pl.ANY)],
        out_specs=vmem,
        scratch_shapes=[
            pltpu.VMEM((steps, NZ, 2, NY, toks, width + LANES), half),
            pltpu.VMEM((3, width, ff), half),
            pltpu.VMEM((4 * toks, ff), half),
            pltpu.VMEM((groups, 2, NY, toks, width), half),
            pltpu.VMEM((groups, NY, toks, width), half),
            pltpu.VMEM((groups, toks, width), half),
            pltpu.VMEM((groups, toks, width), half),
            pltpu.VMEM((groups, toks, width), half),
            pltpu.VMEM((steps, NZ, toks, width), half),
            dma((3,)),
            dma((steps, NZ, 2, NY)),
            dma((steps, NZ, 7)),
            dma((groups,)),
            dma((groups,)),
            dma((groups,)),
            dma((groups,)),
            dma((steps, NZ)),
            dma((groups,)),
        ],
        compiler_params=pltpu.CompilerParams(
            collective_id=0, has_side_effects=True, vmem_limit_bytes=48 * 1024 * 1024
        ),
        cost_estimate=pl.CostEstimate(
            flops=6 * rows * width * ff, bytes_accessed=6 * width * ff, transcendentals=rows * ff
        ),
    )(tokens, norm_gain.reshape(1, width), expert_ids, gate_probs, expert_weights)


def solution(mesh):
    in_specs = (
        P(None, ("grp", "ep", "dp"), None),
        P(),
        P(None, ("grp", "ep", "dp"), None),
        P(None, ("grp", "ep", "dp"), None),
        P(("ep", "dp"), None, None, None),
    )
    out_specs = P(None, ("grp", "ep", "dp"), None)
    small = mesh.shape["ep"] == NZ * NY and mesh.shape["dp"] == 2
    shards = kernel_form if small else gather_scatter_form
    return jax.shard_map(shards, mesh=mesh, in_specs=in_specs, out_specs=out_specs, check_vma=False)
```
